32 devices in a mesh: parts: 2 (over x), seq: 16 (over z, y, core).
Axes of the slice: x: 2, y: 2, z: 4, core: 2. Of those that a mesh axis runs over, the one named last changes fastest.
Arguments:
- frames: bfloat16 [8, 1024, 1024], P('parts', 'seq'), parts along dimension 0, may hold values from -10 to 10
- conv_weight: bfloat16 [128, 64, 1024], P('seq'), may hold values from -0.0625 to 0.0625
- conv_bias: float32 [1024], replicated, may hold values from -1 to 1
- w_qkv: bfloat16 [1024, 3, 16, 64], replicated, may hold values from -1 to 1
- w_out: bfloat16 [16, 64, 1024], replicated, may hold values from -1.5 to 1.5
Outputs:
- targets: bfloat16 [8, 1024, 1024], P('parts', 'seq'), parts along dimension 0
The draws below stay inside these ranges and needn't reach their ends.
There are 2 independent parts, one for each index of `parts`. The reference program is written for one: setup_inputs(seed, part) draws one part's arguments, and reference() takes and returns one part's arrays. A program takes and returns all parts, laid end to end along the dimension named above; an argument that names none is the same for every part. Nothing has to cross between parts.
All inputs are finite; a program needn't handle non-finite values.
Results may differ from the reference program's by a relative error of at most 0.012.
The reference program's roundings to bfloat16 on the way (of `mixed`, `qkv`, `probs` and `context`) count: a program that leaves them out, or rounds other values in their place, can miss the bound.
Values may be sent and summed in bfloat16 or wider, within the bound.
No kernel may reach another device: no remote copies, remote signals or barrier semaphores. Data moves between devices by JAX's collectives and lax.ppermute only.
A program may use at most 192 MiB of HBM per device.

```python
import math
import jax
import jax.numpy as jnp
from jax import lax

D = 1024
HEADS = 16
GROUPS = 16
KERNEL = 128
HEAD = 64
REC = 4
LENGTH = 1024


def draw_frames(key, part):
    first = jax.random.fold_in(key, 0)
    return jnp.clip(jax.random.normal(first, (REC, LENGTH, D), jnp.float32), -6.0, 6.0).astype(jnp.bfloat16)


def draw_w_qkv(key, part):
    base = jax.random.normal(key, (D, 3, HEADS, HEAD), jnp.float32)
    base = jnp.clip(base, -6.0, 6.0) / math.sqrt(D)
    return base.astype(jnp.bfloat16)


def level_of(stream_key, shape, cuts, smallest, high):
    loudness = 1.0
    for dim, parts in cuts:
        steps = jax.random.uniform(jax.random.fold_in(jax.random.fold_in(stream_key, 6), dim), (parts,), jnp.float32, smallest / len(cuts), high / len(cuts))
        loudness = loudness * jnp.repeat(jnp.exp(steps), shape[dim] // parts).reshape((-1,) + (1,) * (len(shape) - 1 - dim))
    return loudness


def gaussian(own_key, shape, width, limit, cuts=(), kind=jnp.bfloat16):
    entries = jax.random.normal(own_key, shape, jnp.float32) * width
    if len(cuts) > 0:
        entries = level_of(own_key, shape, cuts, -0.22, 0.18) * entries
    return jnp.clip(entries, min=-limit, max=limit).astype(kind)


def setup_inputs(seed: int = 0, part: int = 0) -> dict:
    streams_of = jax.random.split(jax.random.key(seed), 6)
    part_keys = jax.random.split(jax.random.fold_in(streams_of[5], part), 6)
    return {
        "frames": draw_frames(jax.random.fold_in(jax.random.fold_in(streams_of[5], part), 71), part),
        "conv_weight": gaussian(streams_of[1], (KERNEL, D // GROUPS, D), (KERNEL * D // GROUPS) ** -0.5, 0.0625, ((0, 16),)),
        "conv_bias": jnp.clip(jax.random.uniform(streams_of[2], (D,), jnp.float32, -1.0, 1.0), -1.0, 1.0),
        "w_qkv": draw_w_qkv(jax.random.fold_in(streams_of[5], 71), part),
        "w_out": gaussian(streams_of[4], (HEADS, HEAD, D), 0.25, 1.5),
    }


def reference(frames, conv_weight, conv_bias, w_qkv, w_out):
    half = KERNEL // 2
    group_width = D // GROUPS
    padded = jnp.pad(frames, ((0, 0), (half, half), (0, 0))).astype(jnp.float32)
    grouped = padded.reshape(REC, LENGTH + KERNEL, GROUPS, group_width)
    kernel = conv_weight.astype(jnp.float32).reshape(KERNEL, group_width, GROUPS, group_width)

    def add_tap(tap, total):
        window = lax.dynamic_slice_in_dim(grouped, tap, LENGTH, 1)
        piece = lax.dynamic_index_in_dim(kernel, tap, 0, keepdims=False)
        return total + jnp.einsum('btgi,igo->btgo', window, piece)
    empty = jnp.zeros((REC, LENGTH, GROUPS, group_width), jnp.float32)
    conv = lax.fori_loop(0, KERNEL, add_tap, empty).reshape(REC, LENGTH, D) + conv_bias
    mixed = (frames.astype(jnp.float32) + jax.nn.gelu(conv)).astype(jnp.bfloat16)
    qkv = jnp.einsum('btd,dshe->bhtse', mixed.astype(jnp.float32), w_qkv.astype(jnp.float32)).astype(jnp.bfloat16)
    grid = qkv.reshape(REC * HEADS, LENGTH, 3, HEAD)
    scale = HEAD ** (-0.5)
    block = min(LENGTH, 512)

    def one(item):
        query = item[:, 0]
        keys = item[:, 1]
        values = item[:, 2]

        def rows(query_block):
            scores = jnp.einsum('qe,ke->qk', query_block.astype(jnp.float32), keys.astype(jnp.float32)) * scale
            top = lax.optimization_barrier(jnp.max(scores, axis=1, keepdims=True))
            weights = jnp.exp(scores - top)
            probs = (weights / lax.optimization_barrier(jnp.sum(weights, axis=1, keepdims=True))).astype(jnp.bfloat16)
            return jnp.dot(probs, values, preferred_element_type=jnp.float32).astype(jnp.bfloat16)
        return lax.map(rows, query.reshape(LENGTH // block, block, HEAD)).reshape(LENGTH, HEAD)
    context = lax.map(one, grid).reshape(REC, HEADS, LENGTH, HEAD)
    out = jnp.einsum('bhte,hed->btd', context.astype(jnp.float32), w_out.astype(jnp.float32))
    total = mixed.astype(jnp.float32) + out
    mean = lax.optimization_barrier(jnp.mean(total, axis=2, keepdims=True))
    centered = total - mean
    var = lax.optimization_barrier(jnp.mean(centered * centered, axis=2, keepdims=True))
    return (centered / jnp.sqrt(var + 1e-05)).astype(jnp.bfloat16)
```

```python
import math

import jax
import jax.numpy as jnp
from jax import lax
from jax.experimental import pallas as pl
from jax.experimental.pallas import tpu as pltpu
from jax.sharding import PartitionSpec as P

GROUPS = 16
KERNEL = 128
LANES = 128


def params(limit=60 << 20):
    return pltpu.CompilerParams(vmem_limit_bytes=limit)


def whole_spec(count):
    return [pl.BlockSpec(memory_space=pltpu.VMEM)] * count


def swap(x):
    return jnp.concatenate([x[:, LANES // 2 :], x[:, : LANES // 2]], axis=1)


def low_lanes(rows):
    return lax.broadcasted_iota(jnp.int32, (rows, LANES), 1) < LANES // 2


def halves(low, first, second):
    return jnp.where(low, first, swap(second)), jnp.where(low, swap(first), second)


def pack_kernel(frames, weight, out):
    rec, rows, width = frames.shape
    taps = weight.shape[0]
    low = low_lanes(rows)
    for tile in range(width // LANES):
        columns = slice(tile * LANES, (tile + 1) * LANES)
        at = 0
        for source, count in ((frames, rec), (weight, taps)):
            for item in range(count // 2):
                first = source[item, :, columns].astype(jnp.float32)
                second = source[item + count // 2, :, columns].astype(jnp.float32)
                even, odd = halves(low, first, second)
                out[2 * tile, at : at + rows, :] = even.astype(jnp.bfloat16)
                out[2 * tile + 1, at : at + rows, :] = odd.astype(jnp.bfloat16)
                at += rows


def pack(frames, weight):
    rec, rows, width = frames.shape
    taps = weight.shape[0]
    return pl.pallas_call(
        pack_kernel,
        out_shape=jax.ShapeDtypeStruct((GROUPS, (rec + taps) // 2 * rows, LANES), jnp.bfloat16),
        in_specs=whole_spec(2),
        out_specs=pl.BlockSpec(memory_space=pltpu.VMEM),
        compiler_params=params(),
        name="pack",
    )(frames, weight)


def conv_kernel(place, rec, frame_count, got, bias, out, padded, quads, partial, kernel):
    sources = got.shape[0]
    half = KERNEL // 2
    length = sources * frame_count
    mid = length // 2
    frame_rows = rec // 2 * frame_count
    depth = 2 * LANES
    steps = sources // 2
    me = place[0]
    for pair in range(rec // 2):
        padded[pair, 0:half, :] = jnp.zeros((half, LANES), jnp.float32)
        tail = padded.shape[1] - half - length
        padded[pair, half + length :, :] = jnp.zeros((tail, LANES), jnp.float32)
        for source in range(sources):
            rows = got[source, pair * frame_count : (pair + 1) * frame_count, :]
            start = half + source * frame_count
            padded[pair, start : start + frame_count, :] = rows.astype(jnp.float32)
    for source in range(sources):
        step, side = source // 2, source % 2
        kernel[step * depth : (step + 1) * depth, side * LANES : (side + 1) * LANES] = got[
            source, frame_rows:, :
        ]

    def one(item, carry):
        number = jnp.bitwise_xor(item, me)
        pair = lax.rem(number, rec // 2)
        second = number // (rec // 2)
        span = quads.shape[0]
        chunk = span // 9
        for part in range(9):
            at = part * chunk
            low = low_lanes(chunk)
            shifted = [padded[pair, at + a : at + a + chunk, :] for a in range(4)]
            turned = [swap(x) for x in shifted]
            mine = [jnp.where(second == 0, x, y) for x, y in zip(shifted, turned)]
            other = [jnp.where(second == 0, y, x) for x, y in zip(shifted, turned)]
            for side in range(2):
                tile = jnp.where(low, mine[2 * side], other[2 * side + 1])
                quads[at : at + chunk, side * LANES : (side + 1) * LANES] = tile.astype(jnp.bfloat16)
        rows = partial.shape[0] // 5
        for part in range(5):
            at = part * rows
            left = jnp.concatenate(
                [quads[at + 16 * k : at + 16 * k + rows, :] for k in range(steps)], axis=1
            )
            partial[at : at + rows, :] = jnp.dot(
                left, kernel[...], preferred_element_type=jnp.float32
            )
        piece = mid // 4
        for part in range(4):
            low = low_lanes(piece)
            at = part * piece

            def sums(start):
                u = partial[start : start + piece, :LANES] + partial[start + 8 : start + 8 + piece, LANES:]
                v = partial[start + 4 : start + 4 + piece, :LANES] + partial[start + 12 : start + 12 + piece, LANES:]
                return u, v

            u0, v0 = sums(at)
            u1, v1 = sums(at + mid)
            conv = jnp.where(low, u0, v1) + swap(jnp.where(low, u1, v0)) + bias[...]
            f0 = padded[pair, half + at : half + at + piece, :]
            f1 = padded[pair, half + mid + at : half + mid + at + piece, :]
            own0 = jnp.where(second == 0, f0, swap(f0))
            own1 = jnp.where(second == 0, swap(f1), f1)
            own = jnp.where(low, own0, own1)
            mixed = own + jax.nn.gelu(conv)
            out[item, at : at + piece, :] = mixed.astype(jnp.bfloat16)
        return carry

    lax.fori_loop(0, rec, one, 0)


def conv_group(place, got, bias, rec, frame_count):
    sources = got.shape[0]
    length = sources * frame_count
    span = length + KERNEL
    return pl.pallas_call(
        lambda *refs: conv_kernel(refs[0], rec, frame_count, *refs[1:]),
        out_shape=jax.ShapeDtypeStruct((rec, length // 2, LANES), jnp.bfloat16),
        in_specs=[pl.BlockSpec(memory_space=pltpu.SMEM)] + whole_spec(2),
        out_specs=pl.BlockSpec(memory_space=pltpu.VMEM),
        scratch_shapes=[
            pltpu.VMEM((rec // 2, span + 16, LANES), jnp.float32),
            pltpu.VMEM((span, 2 * LANES), jnp.bfloat16),
            pltpu.VMEM((length + 16, 2 * LANES), jnp.float32),
            pltpu.VMEM((sources * LANES, 2 * LANES), jnp.bfloat16),
        ],
        compiler_params=params(),
        name="conv",
    )(place, got, bias)


def attend_kernel(rec, team, head, frame_count, place, *refs):
    count = rec * team
    chunks = refs[:count]
    w_ref, context, rows_out, mixed, qkv, keys = refs[count:]
    tiles, length, _ = mixed.shape
    mid = length // 2
    mine, member = place[0], place[1]
    core = lax.rem(member, 2)
    low = low_lanes(mid)
    for m in range(rec):
        for pair in range(team // 2):
            first = chunks[m * team + 2 * pair][...].astype(jnp.float32)
            second = chunks[m * team + 2 * pair + 1][...].astype(jnp.float32)
            even = jnp.where(core == 0, first, second)
            odd = jnp.where(core == 0, second, first)
            tile = jnp.bitwise_xor(mine, m) * (team // 2) + jnp.bitwise_xor(member // 2, pair)
            top, bottom = halves(low, even, odd)
            mixed[tile, :mid, :] = top.astype(jnp.bfloat16)
            mixed[tile, mid:, :] = bottom.astype(jnp.bfloat16)
    width = qkv.shape[1] // 3
    rows = 256
    low = low_lanes(rows)

    def project(part, carry):
        at = pl.multiple_of(part * rows, rows)
        left = jnp.concatenate([mixed[t, pl.ds(at, rows), :] for t in range(tiles)], axis=1)
        made = jnp.dot(left, w_ref[...], preferred_element_type=jnp.float32)
        qkv[pl.ds(at, rows), :] = made.astype(jnp.bfloat16)
        for pair in range(width // LANES):
            key = made[:, width + pair * LANES : width + (pair + 1) * LANES]
            keys[2 * pair, pl.ds(at, rows), :] = jnp.where(low, key, 0.0).astype(jnp.bfloat16)
            keys[2 * pair + 1, pl.ds(at, rows), :] = jnp.where(low, 0.0, key).astype(jnp.bfloat16)
        return carry

    lax.fori_loop(0, length // rows, project, 0)
    block = team * frame_count
    for z in range(rec):
        at = pl.multiple_of(z * block + member * frame_count, frame_count)
        for t in range(tiles):
            rows_out[z * frame_count : (z + 1) * frame_count, t * LANES : (t + 1) * LANES] = mixed[
                t, pl.ds(at, frame_count), :
            ]
    factor = head**-0.5 * math.log2(math.e)
    query_rows = rec * frame_count
    low = low_lanes(query_rows)

    def one(q, carry):
        who = jnp.bitwise_xor(member, q)
        starts = [pl.multiple_of(z * block + who * frame_count, frame_count) for z in range(rec)]
        for pair in range(width // LANES):
            columns = slice(pair * LANES, (pair + 1) * LANES)
            query = jnp.concatenate([qkv[pl.ds(s, frame_count), columns] for s in starts], axis=0)
            value = qkv[:, 2 * width + pair * LANES : 2 * width + (pair + 1) * LANES]
            made = []
            for side in range(2):
                scores = lax.dot_general(
                    query, keys[2 * pair + side], (((1,), (1,)), ((), ())),
                    preferred_element_type=jnp.float32,
                )
                top = jnp.max(scores, axis=1, keepdims=True)
                weights = jnp.exp2((scores - top) * factor)
                share = 1.0 / jnp.sum(weights, axis=1, keepdims=True)
                probs = (weights * share).astype(jnp.bfloat16)
                made.append(jnp.dot(probs, value, preferred_element_type=jnp.float32))
            context[q, :, columns] = jnp.where(low, made[0], made[1]).astype(jnp.bfloat16)
        return carry

    lax.fori_loop(0, team, one, 0)


def attend(place, chunks, w, rec, team, head, frame_count):
    depth, columns = w.shape
    length = 2 * chunks[0].shape[0]
    width = columns // 3
    rows = rec * frame_count
    return pl.pallas_call(
        lambda *refs: attend_kernel(rec, team, head, frame_count, *refs),
        out_shape=[
            jax.ShapeDtypeStruct((team, rows, width), jnp.bfloat16),
            jax.ShapeDtypeStruct((rows, depth), jnp.bfloat16),
        ],
        in_specs=[pl.BlockSpec(memory_space=pltpu.SMEM)] + whole_spec(len(chunks) + 1),
        out_specs=whole_spec(2),
        scratch_shapes=[
            pltpu.VMEM((depth // LANES, length, LANES), jnp.bfloat16),
            pltpu.VMEM((length, columns), jnp.bfloat16),
            pltpu.VMEM((width // head, length, LANES), jnp.bfloat16),
        ],
        compiler_params=params(),
        name="attend",
    )(place, *chunks, w)


def output_kernel(rec, place, *refs):
    *contexts, w_ref, mixed, out = refs
    mine, member = place[0], place[1]
    width = contexts[0].shape[1]
    total = mixed[...].astype(jnp.float32)
    for q, context in enumerate(contexts):
        at = pl.multiple_of(jnp.bitwise_xor(member, q) * width, width)
        total = total + jnp.dot(
            context[...], w_ref[pl.ds(at, width), :], preferred_element_type=jnp.float32
        )
    mean = jnp.mean(total, axis=1, keepdims=True)
    centered = total - mean
    var = jnp.mean(centered * centered, axis=1, keepdims=True)
    made = (centered / jnp.sqrt(var + 1e-05)).astype(jnp.bfloat16)
    rows = out.shape[1]
    for z in range(rec):
        out[jnp.bitwise_xor(mine, z)] = made[z * rows : (z + 1) * rows, :]


def output(place, contexts, w, mixed, rec):
    rows, depth = mixed.shape
    return pl.pallas_call(
        lambda *refs: output_kernel(rec, *refs),
        out_shape=jax.ShapeDtypeStruct((rec, rows // rec, depth), jnp.bfloat16),
        in_specs=[pl.BlockSpec(memory_space=pltpu.SMEM)] + whole_spec(len(contexts) + 2),
        out_specs=pl.BlockSpec(memory_space=pltpu.VMEM),
        compiler_params=params(),
        name="output",
    )(place, *contexts, w, mixed)


def gather_kernel(place, *refs):
    *parts, out = refs
    for m, part in enumerate(parts):
        out[jnp.bitwise_xor(place[0], m)] = part[...]


def gather(place, parts):
    return pl.pallas_call(
        gather_kernel,
        out_shape=jax.ShapeDtypeStruct((len(parts),) + parts[0].shape, parts[0].dtype),
        in_specs=[pl.BlockSpec(memory_space=pltpu.SMEM)] + whole_spec(len(parts)),
        out_specs=pl.BlockSpec(memory_space=pltpu.VMEM),
        compiler_params=params(),
        name="gather",
    )(place, *parts)


def exchange(x, devices, mask):
    return lax.ppermute(x, "seq", [(s, s ^ mask) for s in range(devices)])


def fast_body(frames, conv_weight, conv_bias, w_qkv, w_out):
    rec, frame_count, width = frames.shape
    devices = lax.axis_size("seq")
    group_width = width // GROUPS
    heads, head = w_qkv.shape[2:]
    team = devices // rec
    per_dev = heads // team
    me = lax.axis_index("seq")
    mine, member = me // team, lax.rem(me, team)
    place = jnp.stack([mine, member]).astype(jnp.int32)

    got = lax.all_to_all(pack(frames, conv_weight), "seq", split_axis=0, concat_axis=0, tiled=True)
    bias = lax.dynamic_slice_in_dim(conv_bias, me * group_width, group_width)
    bias = jnp.concatenate([bias, bias]).reshape(1, LANES)
    mixed = conv_group(place, got, bias, rec, frame_count)

    own_w = lax.dynamic_slice_in_dim(w_qkv, member * per_dev, per_dev, axis=2)
    own_w = own_w.reshape(width, 3 * per_dev * head)
    across = [mixed[0]] + [exchange(mixed[m], devices, m * team) for m in range(1, rec)]
    chunks = []
    for piece in across:
        known = [piece]
        step = team // 2
        shared = {0: piece}
        while step:
            for q in list(shared):
                shared[q ^ step] = exchange(shared[q], devices, step)
            step //= 2
        chunks += [shared[q] for q in range(team)]
    context, own_rows = attend(place, chunks, own_w, rec, team, head, frame_count)
    contexts = [context[0]] + [exchange(context[q], devices, q) for q in range(1, team)]
    made = output(place, contexts, w_out.reshape(heads * head, width), own_rows, rec)
    parts = [made[0]] + [exchange(made[m], devices, m * team) for m in range(1, rec)]
    return gather(place, parts)


def conv_part(source, kernel, groups):
    return lax.conv_general_dilated(
        source,
        kernel,
        (1,),
        "VALID",
        dimension_numbers=("NWC", "WIO", "NWC"),
        feature_group_count=groups,
        preferred_element_type=jnp.float32,
    )


def body(frames, conv_weight, conv_bias, w_qkv, w_out):
    rec, frame_count, width = frames.shape
    devices = lax.axis_size("seq")
    group_width = width // GROUPS
    half = KERNEL // 2
    blocks = devices // GROUPS
    per_dev = rec // blocks
    tap_count = conv_weight.shape[0]
    spread = conv_weight.reshape(tap_count, group_width, 1, GROUPS, group_width)
    spread = jnp.broadcast_to(spread, (tap_count, group_width, blocks, GROUPS, group_width))
    spread = spread.reshape(tap_count, group_width, devices, group_width)
    kernel = lax.all_to_all(spread, "seq", split_axis=2, concat_axis=0, tiled=True).reshape(
        KERNEL, group_width, group_width
    )
    arranged = frames.reshape(blocks, per_dev, frame_count, GROUPS, group_width)
    arranged = jnp.transpose(arranged, (0, 3, 1, 2, 4)).reshape(
        devices, per_dev, frame_count, group_width
    )
    length = frame_count * devices
    inputs = lax.all_to_all(arranged, "seq", split_axis=0, concat_axis=2, tiled=True).reshape(
        per_dev, length, group_width
    )
    padded = jnp.pad(inputs, ((0, 0), (half, half - 1), (0, 0)))
    conv = conv_part(padded, kernel, 1)
    group_index = lax.axis_index("seq") % GROUPS
    bias = lax.dynamic_slice_in_dim(conv_bias, group_index * group_width, group_width)
    local = (inputs.astype(jnp.float32) + jax.nn.gelu(conv + bias)).astype(jnp.bfloat16)
    sending = local.reshape(1, per_dev, devices, frame_count, group_width)
    returned = lax.all_to_all(sending, "seq", split_axis=2, concat_axis=0, tiled=True)
    returned = returned.reshape(blocks, GROUPS, per_dev, frame_count, group_width)
    mixed = jnp.transpose(returned, (0, 2, 3, 1, 4)).reshape(rec, frame_count, width)
    heads = w_qkv.shape[2]
    head = w_qkv.shape[3]
    items = rec * heads // devices
    projected = jnp.einsum(
        "btd,dshe->bhtse", mixed, w_qkv, preferred_element_type=jnp.float32
    ).astype(jnp.bfloat16)
    packed = projected.reshape(devices, items, frame_count, 3 * head)
    scale = head ** (-0.5)
    portion = lax.all_to_all(packed, "seq", split_axis=0, concat_axis=2, tiled=True)
    count = portion.shape[1]
    length = portion.shape[2]
    grid = portion.reshape(count, length, 3, head)
    block = math.gcd(length, 512)

    def one(item):
        query = item[:, 0]
        keys = item[:, 1]
        values = item[:, 2]

        def rows(query_block):
            scores = (
                jnp.einsum("qe,ke->qk", query_block, keys, preferred_element_type=jnp.float32)
                * scale
            )
            top = jnp.max(scores, axis=1, keepdims=True)
            weights = jnp.exp(scores - top)
            probs = (weights / jnp.sum(weights, axis=1, keepdims=True)).astype(jnp.bfloat16)
            return jnp.dot(probs, values, preferred_element_type=jnp.float32).astype(jnp.bfloat16)

        return lax.map(rows, query.reshape(length // block, block, head)).reshape(length, head)

    attended = lax.map(one, grid)
    context = lax.all_to_all(attended[None], "seq", split_axis=2, concat_axis=0, tiled=True)
    context = context.reshape(rec, heads, frame_count, head)
    out = jnp.einsum("bhte,hed->btd", context, w_out, preferred_element_type=jnp.float32)
    total = mixed.astype(jnp.float32) + out
    mean = jnp.mean(total, axis=2, keepdims=True)
    centered = total - mean
    var = jnp.mean(centered * centered, axis=2, keepdims=True)
    return (centered / jnp.sqrt(var + 1e-05)).astype(jnp.bfloat16)


def solution(mesh):
    devices = mesh.shape["seq"]
    return jax.shard_map(
        fast_body if devices == GROUPS else body,
        mesh=mesh,
        in_specs=(P("parts", "seq", None), P("seq", None, None), P(), P(), P()),
        out_specs=P("parts", "seq", None),
        check_vma=False,
    )
```

```python
import math

import jax
import jax.numpy as jnp
from jax import lax
from jax.experimental import pallas as pl
from jax.experimental.pallas import tpu as pltpu
from jax.sharding import PartitionSpec as P

GROUPS = 16
KERNEL = 128
LANES = 128


def params(limit=20 << 20):
    return pltpu.CompilerParams(vmem_limit_bytes=limit)


def whole_spec(count):
    return [pl.BlockSpec(memory_space=pltpu.VMEM)] * count


def swap(x):
    return jnp.concatenate([x[:, LANES // 2 :], x[:, : LANES // 2]], axis=1)


def low_lanes(rows):
    return lax.broadcasted_iota(jnp.int32, (rows, LANES), 1) < LANES // 2


def halves(low, first, second):
    return jnp.where(low, first, swap(second)), jnp.where(low, swap(first), second)


def pack_kernel(frames, weight, out):
    rec, rows, width = frames.shape
    taps = weight.shape[0]
    low = low_lanes(rows)
    for tile in range(width // LANES):
        columns = slice(tile * LANES, (tile + 1) * LANES)
        at = 0
        for source, count in ((frames, rec), (weight, taps)):
            for item in range(count // 2):
                first = source[item, :, columns].astype(jnp.float32)
                second = source[item + count // 2, :, columns].astype(jnp.float32)
                even, odd = halves(low, first, second)
                out[2 * tile, at : at + rows, :] = even.astype(jnp.bfloat16)
                out[2 * tile + 1, at : at + rows, :] = odd.astype(jnp.bfloat16)
                at += rows


def pack(frames, weight):
    rec, rows, width = frames.shape
    taps = weight.shape[0]
    return pl.pallas_call(
        pack_kernel,
        out_shape=jax.ShapeDtypeStruct((GROUPS, (rec + taps) // 2 * rows, LANES), jnp.bfloat16),
        in_specs=whole_spec(2),
        out_specs=pl.BlockSpec(memory_space=pltpu.VMEM),
        compiler_params=params(),
        name="pack",
    )(frames, weight)


def prepare_kernel(rec, frame_count, got, quads, own, kernel, padded):
    sources = got.shape[0]
    half = KERNEL // 2
    length = sources * frame_count
    mid = length // 2
    frame_rows = rec // 2 * frame_count
    depth = 2 * LANES
    for source in range(sources):
        step, side = source // 2, source % 2
        kernel[step * depth : (step + 1) * depth, side * LANES : (side + 1) * LANES] = got[
            source, frame_rows:, :
        ]
    padded[0:half, :] = jnp.zeros((half, LANES), jnp.float32)
    padded[half + length :, :] = jnp.zeros((padded.shape[0] - half - length, LANES), jnp.float32)
    span = quads.shape[1]
    chunk = span // 9

    def one(pair, carry):
        at = pl.multiple_of(pair * frame_count, frame_count)
        for source in range(sources):
            start = half + source * frame_count
            padded[start : start + frame_count, :] = got[source, pl.ds(at, frame_count), :].astype(
                jnp.float32
            )
        for part in range(9):
            at = part * chunk
            low = low_lanes(chunk)
            shifted = [padded[at + a : at + a + chunk, :] for a in range(4)]
            for side in range(2):
                first, second = halves(low, shifted[2 * side], shifted[2 * side + 1])
                columns = slice(side * LANES, (side + 1) * LANES)
                quads[pair, at : at + chunk, columns] = first.astype(jnp.bfloat16)
                quads[pair + rec // 2, at : at + chunk, columns] = second.astype(jnp.bfloat16)
        low = low_lanes(mid)
        f0 = padded[half : half + mid, :]
        f1 = padded[half + mid : half + length, :]
        first, second = halves(low, f0, f1)
        own[pair] = first.astype(jnp.bfloat16)
        own[pair + rec // 2] = second.astype(jnp.bfloat16)
        return carry

    lax.fori_loop(0, rec // 2, one, 0)


def prepare(got, rec, frame_count):
    sources = got.shape[0]
    length = sources * frame_count
    span = length + KERNEL
    return pl.pallas_call(
        lambda *refs: prepare_kernel(rec, frame_count, *refs),
        out_shape=[
            pltpu.VMEM((rec, span, 2 * LANES), jnp.bfloat16),
            pltpu.VMEM((rec, length // 2, LANES), jnp.bfloat16),
            pltpu.VMEM((sources * LANES, 2 * LANES), jnp.bfloat16),
        ],
        in_specs=whole_spec(1),
        out_specs=whole_spec(3),
        scratch_shapes=[pltpu.VMEM((span + 16, LANES), jnp.float32)],
        compiler_params=params(),
        name="prepare",
    )(got)


def conv_kernel(m, place, quads, own, kernel, bias, out, partial):
    mid = own.shape[1]
    number = jnp.bitwise_xor(m, place[0])
    steps = kernel.shape[0] // (2 * LANES)
    rows = partial.shape[0] // 5
    for part in range(5):
        at = part * rows
        left = jnp.concatenate(
            [quads[number, at + 16 * k : at + 16 * k + rows, :] for k in range(steps)], axis=1
        )
        partial[at : at + rows, :] = jnp.dot(left, kernel[...], preferred_element_type=jnp.float32)
    piece = mid // 8
    low = low_lanes(piece)

    def sums(start):
        u = partial[start : start + piece, :LANES] + partial[start + 8 : start + 8 + piece, LANES:]
        v = partial[start + 4 : start + 4 + piece, :LANES]
        return u, v + partial[start + 12 : start + 12 + piece, LANES:]

    for part in range(8):
        at = part * piece
        u0, v0 = sums(at)
        u1, v1 = sums(at + mid)
        conv = jnp.where(low, u0, v1) + swap(jnp.where(low, u1, v0)) + bias[...]
        mixed = own[number, at : at + piece, :].astype(jnp.float32) + jax.nn.gelu(conv)
        out[at : at + piece, :] = mixed.astype(jnp.bfloat16)


def conv_group(m, place, quads, own, kernel, bias):
    return pl.pallas_call(
        lambda *refs: conv_kernel(m, *refs),
        out_shape=jax.ShapeDtypeStruct(own.shape[1:], jnp.bfloat16),
        in_specs=[pl.BlockSpec(memory_space=pltpu.SMEM)] + whole_spec(4),
        out_specs=pl.BlockSpec(memory_space=pltpu.VMEM),
        scratch_shapes=[pltpu.VMEM((2 * own.shape[1] + 16, 2 * LANES), jnp.float32)],
        compiler_params=params(),
        name=f"conv{m}",
    )(place, quads, own, kernel, bias)


def attend_kernel(rec, team, head, frame_count, place, *refs):
    count = rec * team
    chunks = refs[:count]
    w_hbm = refs[count]
    contexts = refs[count + 1 : count + 1 + team]
    rows_out, mixed, qkv, w_ref, even_scores, odd_scores, even_probs, odd_probs, sem = refs[
        count + 1 + team :
    ]
    tiles, length, _ = mixed.shape
    mid = length // 2
    mine, member = place[0], place[1]
    mine_heads = w_ref.shape[1]
    fetch = pltpu.make_async_copy(
        w_hbm.at[:, pl.ds(member * mine_heads, mine_heads)], w_ref, sem
    )
    fetch.start()
    core = lax.rem(member, 2)
    low = low_lanes(mid)
    for m in range(rec):
        for pair in range(team // 2):
            first = chunks[m * team + 2 * pair][...]
            second = chunks[m * team + 2 * pair + 1][...]
            even = jnp.where(core == 0, first, second)
            odd = jnp.where(core == 0, second, first)
            tile = jnp.bitwise_xor(mine, m) * (team // 2) + jnp.bitwise_xor(member // 2, pair)
            top, bottom = halves(low, even, odd)
            mixed[tile, :mid, :] = top
            mixed[tile, mid:, :] = bottom
    fetch.wait()
    width = mine_heads * head
    rows = 256

    def project(part, carry):
        at = pl.multiple_of(part * rows, rows)
        left = jnp.concatenate([mixed[t, pl.ds(at, rows), :] for t in range(tiles)], axis=1)
        made = lax.dot_general(
            left,
            w_ref[...].reshape(3 * width, tiles * LANES),
            (((1,), (1,)), ((), ())),
            preferred_element_type=jnp.float32,
        )
        qkv[pl.ds(at, rows), :] = made.astype(jnp.bfloat16)
        return carry

    lax.fori_loop(0, length // rows, project, 0)
    block = team * frame_count
    for z in range(rec):
        at = pl.multiple_of(z * block + member * frame_count, frame_count)
        for t in range(tiles):
            rows_out[z * frame_count : (z + 1) * frame_count, t * LANES : (t + 1) * LANES] = mixed[
                t, pl.ds(at, frame_count), :
            ]
    factor = head**-0.5 * math.log2(math.e)
    query_rows = rec * frame_count
    low = low_lanes(query_rows)
    strip = 32

    def scores_of(q, number, scores):
        who = jnp.bitwise_xor(member, q)
        pair, side = number // 2, number % 2
        columns = slice(pair * LANES, (pair + 1) * LANES)
        starts = [pl.multiple_of(z * block + who * frame_count, frame_count) for z in range(rec)]
        query = jnp.concatenate([qkv[pl.ds(s, frame_count), columns] for s in starts], axis=0)
        query = jnp.where(low == (side == 0), query, jnp.zeros_like(query))
        key = qkv[:, width + pair * LANES : width + (pair + 1) * LANES]
        scores[...] = lax.dot_general(
            query, key, (((1,), (1,)), ((), ())), preferred_element_type=jnp.float32
        )

    def soften(scores, probs):
        for at in range(0, query_rows, strip):
            own = scores[at : at + strip, :]
            top = jnp.max(own, axis=1, keepdims=True)
            weights = jnp.exp2((own - top) * factor)
            share = 1.0 / jnp.sum(weights, axis=1, keepdims=True)
            probs[at : at + strip, :] = (weights * share).astype(jnp.bfloat16)

    def one(q, carry):
        made = []
        for number in range(mine_heads):
            now, later = (even_scores, odd_scores) if number % 2 == 0 else (odd_scores, even_scores)
            probs = even_probs if number % 2 == 0 else odd_probs
            if number + 1 < mine_heads:
                scores_of(q, number + 1, later)
            else:
                scores_of(jnp.minimum(q + 1, team - 1), 0, later)
            soften(now, probs)
            pair = number // 2
            value = qkv[:, 2 * width + pair * LANES : 2 * width + (pair + 1) * LANES]
            made.append(jnp.dot(probs[...], value, preferred_element_type=jnp.float32))
        for pair in range(mine_heads // 2):
            joined = jnp.where(low, made[2 * pair], made[2 * pair + 1]).astype(jnp.bfloat16)
            for other in range(team):

                @pl.when(q == other)
                def _():
                    contexts[other][:, pair * LANES : (pair + 1) * LANES] = joined

        return carry

    scores_of(0, 0, even_scores)
    lax.fori_loop(0, team, one, 0)


def attend(place, chunks, w, rec, team, frame_count):
    heads, head, depth = w.shape[1:]
    length = 2 * chunks[0].shape[0]
    mine = heads // team
    width = mine * head
    rows = rec * frame_count
    made = pl.pallas_call(
        lambda *refs: attend_kernel(rec, team, head, frame_count, *refs),
        out_shape=[jax.ShapeDtypeStruct((rows, width), jnp.bfloat16)] * team
        + [jax.ShapeDtypeStruct((rows, depth), jnp.bfloat16)],
        in_specs=[pl.BlockSpec(memory_space=pltpu.SMEM)]
        + whole_spec(len(chunks))
        + [pl.BlockSpec(memory_space=pl.ANY)],
        out_specs=whole_spec(team + 1),
        scratch_shapes=[
            pltpu.VMEM((depth // LANES, length, LANES), jnp.bfloat16),
            pltpu.VMEM((length, 3 * width), jnp.bfloat16),
            pltpu.VMEM((3, mine, head, depth), jnp.bfloat16),
            pltpu.VMEM((rows, length), jnp.float32),
            pltpu.VMEM((rows, length), jnp.float32),
            pltpu.VMEM((rows, length), jnp.bfloat16),
            pltpu.VMEM((rows, length), jnp.bfloat16),
            pltpu.SemaphoreType.DMA,
        ],
        compiler_params=params(),
        name="attend",
    )(place, *chunks, w)
    return made[:team], made[team]


def output_kernel(rec, place, *refs):
    *refs, held = refs
    contexts, (w_ref, mixed), outs = refs[: -2 - rec], refs[-2 - rec : -rec], refs[-rec:]
    mine, member = place[0], place[1]
    width = contexts[0].shape[1]
    total = mixed[...].astype(jnp.float32)
    for q, context in enumerate(contexts):
        at = pl.multiple_of(jnp.bitwise_xor(member, q) * width, width)
        total = total + jnp.dot(
            context[...], w_ref[pl.ds(at, width), :], preferred_element_type=jnp.float32
        )
    mean = jnp.mean(total, axis=1, keepdims=True)
    centered = total - mean
    var = jnp.mean(centered * centered, axis=1, keepdims=True)
    made = (centered / jnp.sqrt(var + 1e-05)).astype(jnp.bfloat16)
    held[...] = made
    rows = outs[0].shape[0]
    for m, out in enumerate(outs):
        at = pl.multiple_of(jnp.bitwise_xor(mine, m) * rows, rows)
        out[...] = held[pl.ds(at, rows), :]


def output(place, contexts, w, mixed, rec):
    rows, depth = mixed.shape
    return pl.pallas_call(
        lambda *refs: output_kernel(rec, *refs),
        out_shape=[jax.ShapeDtypeStruct((rows // rec, depth), jnp.bfloat16)] * rec,
        in_specs=[pl.BlockSpec(memory_space=pltpu.SMEM)] + whole_spec(len(contexts) + 2),
        out_specs=whole_spec(rec),
        scratch_shapes=[pltpu.VMEM((rows, depth), jnp.bfloat16)],
        compiler_params=params(),
        name="output",
    )(place, *contexts, w, mixed)


def gather_kernel(place, *refs):
    *parts, out = refs
    for m, part in enumerate(parts):
        out[jnp.bitwise_xor(place[0], m)] = part[...]


def gather(place, parts):
    return pl.pallas_call(
        gather_kernel,
        out_shape=jax.ShapeDtypeStruct((len(parts),) + parts[0].shape, parts[0].dtype),
        in_specs=[pl.BlockSpec(memory_space=pltpu.SMEM)] + whole_spec(len(parts)),
        out_specs=pl.BlockSpec(memory_space=pltpu.VMEM),
        compiler_params=params(),
        name="gather",
    )(place, *parts)


def exchange(x, devices, mask):
    return lax.ppermute(x, "seq", [(s, s ^ mask) for s in range(devices)])


def fast_body(frames, conv_weight, conv_bias, w_qkv, w_out):
    rec, frame_count, width = frames.shape
    devices = lax.axis_size("seq")
    group_width = width // GROUPS
    heads, head = w_qkv.shape[2:]
    team = devices // rec
    me = lax.axis_index("seq")
    mine, member = me // team, lax.rem(me, team)
    place = jnp.stack([mine, member]).astype(jnp.int32)

    got = lax.all_to_all(pack(frames, conv_weight), "seq", split_axis=0, concat_axis=0, tiled=True)
    bias = lax.dynamic_slice_in_dim(conv_bias, me * group_width, group_width)
    bias = jnp.concatenate([bias, bias]).reshape(1, LANES)
    quads, own, kernel = prepare(got, rec, frame_count)
    mixed = [None] * rec
    for m in reversed(range(rec)):
        mixed[m] = conv_group(m, place, quads, own, kernel, bias)

    across = [mixed[0]] + [exchange(mixed[m], devices, m * team) for m in range(1, rec)]
    chunks = []
    for piece in across:
        step = team // 2
        shared = {0: piece}
        while step:
            for q in list(shared):
                shared[q ^ step] = exchange(shared[q], devices, step)
            step //= 2
        chunks += [shared[q] for q in range(team)]
    context, own_rows = attend(
        place, chunks, jnp.transpose(w_qkv, (1, 2, 3, 0)), rec, team, frame_count
    )
    contexts = [context[0]] + [exchange(context[q], devices, q) for q in range(1, team)]
    made = output(place, contexts, w_out.reshape(heads * head, width), own_rows, rec)
    parts = [made[0]] + [exchange(made[m], devices, m * team) for m in range(1, rec)]
    return gather(place, parts)


def conv_part(source, kernel, groups):
    return lax.conv_general_dilated(
        source,
        kernel,
        (1,),
        "VALID",
        dimension_numbers=("NWC", "WIO", "NWC"),
        feature_group_count=groups,
        preferred_element_type=jnp.float32,
    )


def body(frames, conv_weight, conv_bias, w_qkv, w_out):
    rec, frame_count, width = frames.shape
    devices = lax.axis_size("seq")
    group_width = width // GROUPS
    half = KERNEL // 2
    blocks = devices // GROUPS
    per_dev = rec // blocks
    tap_count = conv_weight.shape[0]
    spread = conv_weight.reshape(tap_count, group_width, 1, GROUPS, group_width)
    spread = jnp.broadcast_to(spread, (tap_count, group_width, blocks, GROUPS, group_width))
    spread = spread.reshape(tap_count, group_width, devices, group_width)
    kernel = lax.all_to_all(spread, "seq", split_axis=2, concat_axis=0, tiled=True).reshape(
        KERNEL, group_width, group_width
    )
    arranged = frames.reshape(blocks, per_dev, frame_count, GROUPS, group_width)
    arranged = jnp.transpose(arranged, (0, 3, 1, 2, 4)).reshape(
        devices, per_dev, frame_count, group_width
    )
    length = frame_count * devices
    inputs = lax.all_to_all(arranged, "seq", split_axis=0, concat_axis=2, tiled=True).reshape(
        per_dev, length, group_width
    )
    padded = jnp.pad(inputs, ((0, 0), (half, half - 1), (0, 0)))
    conv = conv_part(padded, kernel, 1)
    group_index = lax.axis_index("seq") % GROUPS
    bias = lax.dynamic_slice_in_dim(conv_bias, group_index * group_width, group_width)
    local = (inputs.astype(jnp.float32) + jax.nn.gelu(conv + bias)).astype(jnp.bfloat16)
    sending = local.reshape(1, per_dev, devices, frame_count, group_width)
    returned = lax.all_to_all(sending, "seq", split_axis=2, concat_axis=0, tiled=True)
    returned = returned.reshape(blocks, GROUPS, per_dev, frame_count, group_width)
    mixed = jnp.transpose(returned, (0, 2, 3, 1, 4)).reshape(rec, frame_count, width)
    heads = w_qkv.shape[2]
    head = w_qkv.shape[3]
    items = rec * heads // devices
    projected = jnp.einsum(
        "btd,dshe->bhtse", mixed, w_qkv, preferred_element_type=jnp.float32
    ).astype(jnp.bfloat16)
    packed = projected.reshape(devices, items, frame_count, 3 * head)
    scale = head ** (-0.5)
    portion = lax.all_to_all(packed, "seq", split_axis=0, concat_axis=2, tiled=True)
    count = portion.shape[1]
    length = portion.shape[2]
    grid = portion.reshape(count, length, 3, head)
    block = math.gcd(length, 512)

    def one(item):
        query = item[:, 0]
        keys = item[:, 1]
        values = item[:, 2]

        def rows(query_block):
            scores = (
                jnp.einsum("qe,ke->qk", query_block, keys, preferred_element_type=jnp.float32)
                * scale
            )
            top = jnp.max(scores, axis=1, keepdims=True)
            weights = jnp.exp(scores - top)
            probs = (weights / jnp.sum(weights, axis=1, keepdims=True)).astype(jnp.bfloat16)
            return jnp.dot(probs, values, preferred_element_type=jnp.float32).astype(jnp.bfloat16)

        return lax.map(rows, query.reshape(length // block, block, head)).reshape(length, head)

    attended = lax.map(one, grid)
    context = lax.all_to_all(attended[None], "seq", split_axis=2, concat_axis=0, tiled=True)
    context = context.reshape(rec, heads, frame_count, head)
    out = jnp.einsum("bhte,hed->btd", context, w_out, preferred_element_type=jnp.float32)
    total = mixed.astype(jnp.float32) + out
    mean = jnp.mean(total, axis=2, keepdims=True)
    centered = total - mean
    var = jnp.mean(centered * centered, axis=2, keepdims=True)
    return (centered / jnp.sqrt(var + 1e-05)).astype(jnp.bfloat16)


def solution(mesh):
    devices = mesh.shape["seq"]
    return jax.shard_map(
        fast_body if devices == GROUPS else body,
        mesh=mesh,
        in_specs=(P("parts", "seq", None), P("seq", None, None), P(), P(), P()),
        out_specs=P("parts", "seq", None),
        check_vma=False,
    )
```
